32 devices in a mesh: grp: 2 (over x), gx: 16 (over z, y, core).
Axes of the slice: x: 2, y: 2, z: 4, core: 2. Of those that a mesh axis runs over, the one named last changes fastest.
Arguments:
- pressure: float32 [256, 1024, 1024], P(('grp', 'gx')), parts along dimension 0, may hold values from -6 to 6
- centres: int32 [8], replicated, may hold values from 1 to 63
- strides: int32 [8], replicated, may hold values from 1 to 127
- kept_bins: int32 [256], replicated, may hold values from 0 to 1023, as said below
Outputs:
- spectrum: float32 [16, 1024, 256], P('grp', 'gx'), parts along dimension 0
The draws below stay inside these ranges and needn't reach their ends.
There are 2 independent parts, one for each index of `grp`. The reference program is written for one: setup_inputs(seed, part) draws one part's arguments, and reference() takes and returns one part's arrays. A program takes and returns all parts, laid end to end along the dimension named above; an argument that names none is the same for every part. Nothing has to cross between parts.
Inputs may be any that keep to these rules, and one draw needn't show every extreme that they name: `kept_bins`: 256 distinct bins, among them 0 and 1023.
All inputs are finite; a program needn't handle non-finite values.
Results may differ from the reference program's by a relative error of at most 0.000092.
Values sent between devices are 32-bit elements; how exact they have to be, the bound alone decides.
No kernel may reach another device: no remote copies, remote signals or barrier semaphores. Data moves between devices by JAX's collectives and lax.ppermute only.
A program may use at most 256 MiB of HBM per device.

```python
import math
import jax
import jax.numpy as jnp
from jax import lax

SNAPS = 128
NX = 1024
NY = 1024
KY = 256
TAPS = 31
BANDS = 8
OUTS = 4


def draw_kept(key, part):
    interior = jax.random.permutation(key, NY - 2)[:KY - 2] + 1
    return jnp.concatenate([jnp.zeros((1,), jnp.int32), interior.astype(jnp.int32), jnp.full((1,), NY - 1, jnp.int32)])


def draw_kept_bins(key, part):
    return draw_kept(key, part)


def with_ends(drawn, key, smallest, high):
    shape = drawn.shape
    place = [jax.random.randint(jax.random.fold_in(key, axis), (), 0, shape[axis]) for axis in range(len(shape))]
    drawn = drawn.at[tuple(place)].set(smallest)
    longest = shape.index(max(shape))
    place[longest] = (place[longest] + 1) % shape[longest]
    return drawn.at[tuple(place)].set(high)


def shard_levels(own_key, dims, shards, low, top_value):
    level = 1.0
    for position, parts in shards:
        heights = jax.random.uniform(jax.random.fold_in(jax.random.fold_in(own_key, 6), position), (parts,), jnp.float32, low / len(shards), top_value / len(shards))
        level = level * jnp.repeat(jnp.exp(heights), dims[position] // parts).reshape((-1,) + (1,) * (len(dims) - 1 - position))
    return level


def bell_draw(key, dims, spread, reach, cuts=(), held_as=jnp.bfloat16):
    values = spread * jax.random.normal(key, dims, jnp.float32)
    if cuts:
        values = values * shard_levels(key, dims, cuts, -0.22, 0.18)
    return jnp.clip(values, -reach, reach).astype(held_as)


def setup_inputs(seed: int = 0, part: int = 0) -> dict:
    key_of = jax.random.split(jax.random.key(seed), 5)
    own_keys = jax.random.split(jax.random.fold_in(key_of[4], part), 5)
    pressure = bell_draw(own_keys[0], (SNAPS, NX, NY), 1.0, 6.0, ((0, 16),), jnp.float32)
    centres = with_ends(jax.random.randint(key_of[1], (BANDS,), 1, SNAPS // 2), jax.random.fold_in(key_of[1], 1), 1, (SNAPS // 2) - 1).astype(jnp.int32)
    strides = with_ends(jax.random.randint(key_of[2], (BANDS,), 1, SNAPS), jax.random.fold_in(key_of[2], 1), 1, SNAPS - 1).astype(jnp.int32)
    kept_bins = draw_kept_bins(jax.random.fold_in(key_of[4], 71), part)
    return {"pressure": pressure, "centres": centres, "strides": strides, "kept_bins": kept_bins}


def filter_bank(centres, strides):
    tap_index = jnp.arange(TAPS, dtype=jnp.int32)
    window = 0.5 - 0.5 * jnp.cos(2.0 * math.pi * (tap_index.astype(jnp.float32) + 1.0) / (TAPS + 1))
    phase_index = (centres[:, None] * tap_index[None, :]) % SNAPS
    phase_angle = -2.0 * math.pi * phase_index.astype(jnp.float32) / SNAPS
    tap_real = window[None, :] * jnp.cos(phase_angle)
    tap_imag = window[None, :] * jnp.sin(phase_angle)
    outputs = jnp.arange(OUTS, dtype=jnp.int32)
    source = (outputs[None, :, None] * strides[:, None, None] + tap_index[None, None, :]) % SNAPS
    onehot = (source[..., None] == jnp.arange(SNAPS, dtype=jnp.int32)).astype(jnp.float32)
    bank_real = jnp.einsum('bk,bjkt->bjt', tap_real, onehot, precision=lax.Precision.HIGHEST)
    bank_imag = jnp.einsum('bk,bjkt->bjt', tap_imag, onehot, precision=lax.Precision.HIGHEST)
    return bank_real.reshape(BANDS * OUTS, SNAPS), bank_imag.reshape(BANDS * OUTS, SNAPS), window


def reference(pressure, centres, strides, kept_bins):
    bank_real, bank_imag, window = filter_bank(centres, strides)
    wsum = jnp.sum(window * window)
    band_real = jnp.einsum('gt,txy->gxy', bank_real, pressure, precision=lax.Precision.HIGHEST)
    band_imag = jnp.einsum('gt,txy->gxy', bank_imag, pressure, precision=lax.Precision.HIGHEST)
    coeffs = jnp.fft.fft2(band_real + 1j * band_imag, axes=(1, 2))
    chosen = coeffs[:, :, kept_bins]
    energy = jnp.real(chosen) ** 2 + jnp.imag(chosen) ** 2
    energy = energy.reshape(BANDS, OUTS, NX, KY)
    spectrum = jnp.mean(energy, axis=1) / (NX * NY * wsum)
    return spectrum.astype(jnp.float32)
```

```python
import functools
import math

import jax
import jax.numpy as jnp
import numpy as np
from jax import lax
from jax.experimental import pallas as pl
from jax.experimental.pallas import tpu as pltpu
from jax.sharding import PartitionSpec as P

KY = 256
TAPS = 31
BANDS = 8
OUTS = 4
LANES = 128
BINS = LANES // 2


def split_bf16(values):
    high = values.astype(jnp.bfloat16)
    low = (values - high.astype(jnp.float32)).astype(jnp.bfloat16)
    return high, low


def split_exact(values):
    high = lax.reduce_precision(values, 8, 7)
    return high.astype(jnp.bfloat16), (values - high).astype(jnp.bfloat16)


def split_host(values):
    values = values.astype(np.float32)
    high = values.astype(jnp.bfloat16)
    low = (values - high.astype(np.float32)).astype(jnp.bfloat16)
    return high, low


def times_i(values):
    lane = lax.broadcasted_iota(jnp.int32, values.shape, 1)
    turned = pltpu.roll(values, BINS, 1)
    return jnp.where(lane < BINS, -turned, turned)


def dot32(left, right):
    return jnp.dot(left, right, preferred_element_type=jnp.float32)


def transform_kernel(radix, share, groups, rank_ref, p_ref, factor_ref, mh_ref, ml_ref, twc_ref, tws_ref, *rest):
    outs, (table_ref, g_ref, f_ref) = rest[:-3], rest[-3:]
    half = groups // 2
    parts = len(outs) // half
    rows = p_ref.shape[1]
    span = rows // radix
    block = 256
    fine = factor_ref.shape[1]

    @pl.when(pl.program_id(0) == 0)
    def _():
        for a in range(p_ref.shape[2] // fine):
            at = slice(a, a + 1)
            both = factor_ref[0, at, :] * factor_ref[2] - factor_ref[1, at, :] * factor_ref[3]
            high, low = split_bf16(both)
            table_ref[a * fine : (a + 1) * fine, :] = jnp.concatenate([high, low], 1)

    @pl.loop(0, rows // block)
    def _(r):
        at = pl.ds(pl.multiple_of(r * block, block), block)
        high, low = split_bf16(p_ref[0, at, :])
        both = dot32(high, table_ref[...]) + dot32(low, table_ref[...])
        g_ref[at, :] = both[:, :LANES] + both[:, LANES:]

    fields = [g_ref[r * span : (r + 1) * span, :] for r in range(radix)]
    if radix == 4:
        a, b = fields[0] + fields[2], fields[0] - fields[2]
        c, d = fields[1] + fields[3], times_i(fields[1] - fields[3])
        fields = [a + c, b - d, a - c, b + d]
    elif radix == 2:
        fields = [fields[0] + fields[1], fields[0] - fields[1]]
    for s, field in enumerate(fields):
        if s:
            field = twc_ref[s] * field + tws_ref[s] * times_i(field)
        high, low = split_bf16(jnp.concatenate([field, times_i(field)], 0))
        right = jnp.concatenate([high, low], 1)
        both = dot32(mh_ref[...], right) + dot32(ml_ref[...], right)
        f_ref[s] = both[:, :LANES] + both[:, LANES:]
    steps = radix // parts
    for k in range(half):
        for h in range(2):
            at = pl.ds(pl.multiple_of((rank_ref[0] ^ (k + h * half)) * share, share), share)
            for s in range(radix):
                first = (h * steps + s % steps) * share
                outs[s // steps * half + k][0, first : first + share, :] = f_ref[s, at, :]


def filter_kernel(places, bank_ref, *rest):
    pieces, out, x_ref = rest[:-2], rest[-2], rest[-1]
    signals, rows = out.shape[1], out.shape[0]
    snaps = x_ref.shape[0] // rows
    for place, piece in zip(places, pieces):
        for t in range(piece.shape[0]):
            first = (place + t) * rows
            x_ref[first : first + rows, :] = piece[t]
    for r in range(rows):
        field = x_ref[pl.ds(r, snaps, stride=rows), :]
        high, low = split_bf16(jnp.concatenate([field, times_i(field)], 0))
        both = dot32(bank_ref[...], jnp.concatenate([high, low], 1))
        both = both[:, :LANES] + both[:, LANES:]
        out[r] = both[:signals] + both[signals:]


def energy_kernel(radix, share, counts, held, scale_ref, *rest):
    fields, out, e_ref = rest[held:-2], rest[-2], rest[-1]
    sides = (fields[: counts[0]], fields[counts[0] :])
    rows = out.shape[1]
    for s in range(radix):
        for i in range(share):
            row = s * share + i
            powers = []
            for side in sides:
                size = side[0].shape[0]
                own, other = side[row // size * 2 : row // size * 2 + 2]
                field = own[row % size] + other[row % size]
                power = field * field
                total = power[:BANDS]
                for j in range(1, OUTS):
                    total = total + power[j * BANDS : (j + 1) * BANDS]
                powers.append(total + pltpu.roll(total, BINS, 1))
            lane = lax.broadcasted_iota(jnp.int32, powers[0].shape, 1)
            x = i * radix + s
            e_ref[x * BANDS : (x + 1) * BANDS, :] = scale_ref[0] * jnp.where(
                lane < BINS, powers[0], powers[1]
            )
    for b in range(BANDS):
        out[b, :, :] = e_ref[pl.ds(b, rows, stride=BANDS), :]


def filter_bank(centres, strides, snaps, times):
    tap_index = jnp.arange(TAPS, dtype=jnp.int32)
    window = 0.5 - 0.5 * jnp.cos(2.0 * math.pi * (tap_index.astype(jnp.float32) + 1.0) / (TAPS + 1))
    phase_index = centres[:, None] * tap_index[None, :] % snaps
    phase_angle = -2.0 * math.pi * phase_index.astype(jnp.float32) / snaps
    tap_real = window[None, :] * jnp.cos(phase_angle)
    tap_imag = window[None, :] * jnp.sin(phase_angle)
    outputs = jnp.arange(OUTS, dtype=jnp.int32)
    source = (outputs[:, None, None] * strides[None, :, None] + tap_index[None, None, :]) % snaps
    chosen = source[..., None] == times
    bank_real = jnp.sum(jnp.where(chosen, tap_real[None, :, :, None], 0.0), axis=2)
    bank_imag = jnp.sum(jnp.where(chosen, tap_imag[None, :, :, None], 0.0), axis=2)
    signals = BANDS * OUTS
    bank = jnp.concatenate(
        [bank_real.reshape(signals, -1), bank_imag.reshape(signals, -1)], axis=1
    )
    return jnp.concatenate(split_exact(bank), axis=0), jnp.sum(window * window)


def bin_factors(kept_bins, ny):
    fine = 32
    lane = jnp.arange(2 * KY, dtype=jnp.int32)
    chunks = kept_bins.reshape(KY // BINS, 1, BINS)
    bins = jnp.concatenate([chunks, chunks], axis=1).reshape(2 * KY)
    quarter = (lane // BINS % 2) * (ny // 4)
    index = jnp.arange(fine, dtype=jnp.int32)[:, None]
    phase = jnp.stack([index * fine * bins, index * bins + quarter], 0) % ny
    angle = phase.astype(jnp.float32) * (2.0 * math.pi / ny)
    cosine, sine = jnp.cos(angle), jnp.sin(angle)
    return jnp.stack([cosine[0], sine[0], cosine[1], sine[1]], 0)


def body(pressure, centres, strides, kept_bins):
    groups = lax.axis_size("gx")
    rank = lax.axis_index("gx")
    local, nx, ny = pressure.shape
    snaps = local * groups
    half = groups // 2
    each = nx // groups
    radix = 4 if each >= 32 else 2 if each >= 16 else 1
    share = each // radix
    span = nx // radix
    signals = BANDS * OUTS

    partner = rank ^ jnp.arange(half, dtype=jnp.int32)
    times = (partner[:, None] * local + jnp.arange(local, dtype=jnp.int32)[None, :]).reshape(-1)
    factors = bin_factors(kept_bins, ny)
    bank, wsum = filter_bank(centres, strides, snaps, times)
    scale = (1.0 / (OUTS * nx * ny * wsum)).reshape(1)
    rank_word = rank.reshape(1).astype(jnp.int32)

    index = np.arange(span, dtype=np.int64)
    angle = 2.0 * np.pi * (index[:, None] * index[None, :] % span) / span
    mh, ml = split_host(np.concatenate([np.cos(angle), np.sin(-angle)], 1))
    twist = 2.0 * np.pi * (np.arange(radix)[:, None] * index[None, :]) / nx
    twist = np.broadcast_to(twist[:, :, None], (radix, span, LANES))
    twc, tws = np.cos(twist).astype(np.float32), np.sin(-twist).astype(np.float32)

    def whole(shape):
        return pl.BlockSpec(shape, lambda *_: (0,) * len(shape))

    def transform(c, factor, first, count, parts):
        size = 2 * each // parts
        return pl.pallas_call(
            functools.partial(transform_kernel, radix, share, groups),
            grid_spec=pltpu.PrefetchScalarGridSpec(
                num_scalar_prefetch=1,
                grid=(count,),
                in_specs=[
                    pl.BlockSpec((1, nx, ny), lambda t, _: (t + first, 0, 0)),
                    pl.BlockSpec((4, factor.shape[1], LANES), lambda t, _: (0, 0, c)),
                    whole(mh.shape),
                    whole(ml.shape),
                    whole(twc.shape),
                    whole(tws.shape),
                ],
                out_specs=[pl.BlockSpec((1, size, LANES), lambda t, _: (t, 0, 0))] * (half * parts),
                scratch_shapes=[
                    pltpu.VMEM((ny, 2 * LANES), jnp.bfloat16),
                    pltpu.VMEM((nx, LANES), jnp.float32),
                    pltpu.VMEM((radix, span, LANES), jnp.float32),
                ],
            ),
            out_shape=[jax.ShapeDtypeStruct((count, size, LANES), jnp.float32)] * (half * parts),
            cost_estimate=pl.CostEstimate(
                flops=count * (8 * nx * ny * LANES + 16 * nx * span * LANES),
                bytes_accessed=count * nx * (ny + LANES) * 4,
                transcendentals=0,
            ),
            name="transform",
        )(rank_word, pressure, factor, mh, ml, twc, tws)

    def filtered(bank, places, pieces, side):
        total = pieces[0].shape[1] // 2
        rows = min(16, total)
        blocks = total // rows
        return pl.pallas_call(
            functools.partial(filter_kernel, places),
            grid=(blocks,),
            in_specs=[whole(bank.shape)]
            + [pl.BlockSpec((x.shape[0], rows, LANES), lambda r: (0, side * blocks + r, 0)) for x in pieces],
            out_specs=pl.BlockSpec((rows, signals, LANES), lambda r: (r, 0, 0)),
            out_shape=jax.ShapeDtypeStruct((total, signals, LANES), jnp.float32),
            scratch_shapes=[pltpu.VMEM((half * local * rows, LANES), jnp.float32)],
            cost_estimate=pl.CostEstimate(
                flops=total * 16 * signals * half * local * LANES,
                bytes_accessed=total * LANES * (half * local + signals) * 4,
                transcendentals=0,
            ),
            name="filter",
        )(bank, *pieces)

    def energy(pair, counts, scale, fields, held):
        return pl.pallas_call(
            functools.partial(energy_kernel, radix, share, counts, len(held)),
            in_specs=[pl.BlockSpec(memory_space=pltpu.SMEM)]
            + [pl.BlockSpec(memory_space=pl.ANY)] * len(held)
            + [whole(x.shape) for x in fields],
            out_specs=pl.BlockSpec((BANDS, each, LANES), lambda _: (0, 0, pair)),
            out_shape=jax.ShapeDtypeStruct((BANDS, each, KY), jnp.float32),
            scratch_shapes=[pltpu.VMEM((each * BANDS, LANES), jnp.float32)],
            grid=(1,),
            input_output_aliases={1: 0} if held else {},
            name="energy",
        )(scale, *held, *fields)

    def swap(value, bits):
        return lax.ppermute(value, "gx", [(i, i ^ bits) for i in range(groups)])

    def exchange(pieces):
        moved = {k: swap(pieces[k], k) for k in reversed(range(1, half))}
        return [pieces[0]] + [moved[k] for k in range(1, half)]

    last_made = [rank_word]

    def in_turn(operand):
        return lax.optimization_barrier((operand, last_made[0]))[0]

    def project(c, pieces_per, parts):
        step = local // pieces_per
        places, found = [], [[] for _ in range(parts)]
        for n in range(pieces_per):
            made = transform(c, in_turn(factors), n * step, step, parts)
            last_made[0] = made[0]
            places += [k * local + n * step for k in range(half)]
            for q in range(parts):
                found[q] += exchange(made[q * half : (q + 1) * half])
        return [(places, pieces) for pieces in found]

    def combine(group, side):
        made = filtered(in_turn(bank), *group, side)
        last_made[0] = made
        return made

    def meet(group):
        made = combine(group, 1)
        return swap(made, half)

    halves = 2 if local % 2 == 0 else 1
    parts = 2 if radix >= 2 else 1
    (zero,) = project(0, halves, 1)
    (one,) = project(1, halves, 1)
    theirs = [meet(zero)]
    (two,) = project(2, 1, 1)
    three = project(3, 1, parts)
    theirs.append(meet(one))
    mine = [combine(zero, 0), combine(one, 0)]
    theirs.append(meet(two))
    mine.append(combine(two, 0))
    out = []
    for n, group in enumerate(three):
        theirs.append(meet(group))
        mine.append(combine(group, 0))
        if n == 0:
            fields = [mine[0], theirs[0], mine[1], theirs[1]]
            out = [energy(0, (2, 2), in_turn(scale), fields, [])]
            last_made[0] = out[0]
    fields = [x for pair in zip(mine[2:], theirs[2:]) for x in pair]
    return energy(1, (2, 2 * parts), in_turn(scale), fields, out)


def solution(mesh):
    return jax.shard_map(
        body,
        mesh=mesh,
        in_specs=(P(("grp", "gx"), None, None), P(), P(), P()),
        out_specs=P("grp", "gx", None),
        check_vma=False,
    )
```

```python
import functools
import math

import jax
import jax.numpy as jnp
import numpy as np
from jax import lax
from jax.experimental import pallas as pl
from jax.experimental.pallas import tpu as pltpu
from jax.sharding import PartitionSpec as P

KY = 256
TAPS = 31
BANDS = 8
OUTS = 4
BINS = 128
LANES = 2 * BINS


def split_bf16(values):
    high = values.astype(jnp.bfloat16)
    low = (values - high.astype(jnp.float32)).astype(jnp.bfloat16)
    return high, low


def split_exact(values):
    high = lax.reduce_precision(values, 8, 7)
    return high.astype(jnp.bfloat16), (values - high).astype(jnp.bfloat16)


def split_host(values):
    values = values.astype(np.float32)
    high = values.astype(jnp.bfloat16)
    low = (values - high.astype(np.float32)).astype(jnp.bfloat16)
    return high, low


def times_i(values):
    return jnp.concatenate([-values[:, BINS:], values[:, :BINS]], 1)


def dot32(left, right):
    return jnp.dot(left, right, preferred_element_type=jnp.float32)


def transform_kernel(parts, share, groups, rank_ref, p_ref, factor_ref, mh_ref, ml_ref, twc_ref, tws_ref, *rest):
    outs, (th_ref, tl_ref, g_ref, f_ref) = rest[:-4], rest[-4:]
    half = groups // 2
    radix = f_ref.shape[0]
    rows = p_ref.shape[1]
    span = rows // radix
    block = 256
    fine = factor_ref.shape[1]

    @pl.when(pl.program_id(0) == 0)
    def _():
        for a in range(p_ref.shape[2] // fine):
            at = slice(a, a + 1)
            both = factor_ref[0, at, :] * factor_ref[2] - factor_ref[1, at, :] * factor_ref[3]
            high, low = split_bf16(both)
            th_ref[a * fine : (a + 1) * fine, :] = high
            tl_ref[a * fine : (a + 1) * fine, :] = low

    @pl.loop(0, rows // block)
    def _(r):
        at = pl.ds(pl.multiple_of(r * block, block), block)
        high, low = split_bf16(p_ref[0, at, :])
        g_ref[at, :] = dot32(high, th_ref[...]) + dot32(high, tl_ref[...]) + dot32(low, th_ref[...])

    fields = [g_ref[r * span : (r + 1) * span, :] for r in range(radix)]
    if radix == 4:
        a, b = fields[0] + fields[2], fields[0] - fields[2]
        c, d = fields[1] + fields[3], times_i(fields[1] - fields[3])
        fields = [a + c, b - d, a - c, b + d]
    elif radix == 2:
        fields = [fields[0] + fields[1], fields[0] - fields[1]]
    for s, field in enumerate(fields):
        if s:
            cosine = jnp.concatenate([twc_ref[s], twc_ref[s]], 1)
            sine = jnp.concatenate([tws_ref[s], tws_ref[s]], 1)
            field = cosine * field + sine * times_i(field)
        high, low = split_bf16(jnp.concatenate([field, times_i(field)], 0))
        f_ref[s] = dot32(mh_ref[...], high) + dot32(mh_ref[...], low) + dot32(ml_ref[...], high)
    for q, part in enumerate(parts):
        for k in range(half):
            for h in range(2):
                at = pl.ds(pl.multiple_of((rank_ref[0] ^ (k + h * half)) * share, share), share)
                for n, s in enumerate(part):
                    first = (h * len(part) + n) * share
                    outs[q * half + k][0, first : first + share, :] = f_ref[s, at, :]


def filter_kernel(places, bank_ref, *rest):
    pieces, (out, re_ref, im_ref) = rest[:-3], rest[-3:]
    signals, rows = out.shape[1], out.shape[0]
    snaps = re_ref.shape[0] // rows
    for place, piece in zip(places, pieces):
        for t in range(piece.shape[0]):
            first = (place + t) * rows
            re_ref[first : first + rows, :] = piece[t, :, :BINS]
            im_ref[first : first + rows, :] = piece[t, :, BINS:]
    for r in range(rows):
        at = pl.ds(r, snaps, stride=rows)
        re, im = re_ref[at, :], im_ref[at, :]
        high, low = split_bf16(
            jnp.concatenate([jnp.concatenate([re, im], 1), jnp.concatenate([-im, re], 1)], 0)
        )
        both = dot32(bank_ref[...], high)
        out[r] = both[:signals] + both[signals:] + dot32(bank_ref[:signals, :], low)


def energy_kernel(parts, share, radix, held, scale_ref, *rest):
    fields, out, e_ref = rest[held:-2], rest[-2], rest[-1]
    rows = out.shape[1]
    for q, part in enumerate(parts):
        own, other = fields[2 * q], fields[2 * q + 1]
        for n, s in enumerate(part):
            for i in range(share):
                field = own[n * share + i] + other[n * share + i]
                power = field * field
                power = power[:, :BINS] + power[:, BINS:]
                total = power[:BANDS]
                for j in range(1, OUTS):
                    total = total + power[j * BANDS : (j + 1) * BANDS]
                x = i * radix + s
                e_ref[x * BANDS : (x + 1) * BANDS, :] = scale_ref[0] * total
    for b in range(BANDS):
        out[b, :, :] = e_ref[pl.ds(b, rows, stride=BANDS), :]


def filter_bank(centres, strides, snaps, times):
    tap_index = jnp.arange(TAPS, dtype=jnp.int32)
    window = 0.5 - 0.5 * jnp.cos(2.0 * math.pi * (tap_index.astype(jnp.float32) + 1.0) / (TAPS + 1))
    phase_index = centres[:, None] * tap_index[None, :] % snaps
    phase_angle = -2.0 * math.pi * phase_index.astype(jnp.float32) / snaps
    tap_real = window[None, :] * jnp.cos(phase_angle)
    tap_imag = window[None, :] * jnp.sin(phase_angle)
    outputs = jnp.arange(OUTS, dtype=jnp.int32)
    source = (outputs[:, None, None] * strides[None, :, None] + tap_index[None, None, :]) % snaps
    chosen = source[..., None] == times
    bank_real = jnp.sum(jnp.where(chosen, tap_real[None, :, :, None], 0.0), axis=2)
    bank_imag = jnp.sum(jnp.where(chosen, tap_imag[None, :, :, None], 0.0), axis=2)
    signals = BANDS * OUTS
    bank = jnp.concatenate(
        [bank_real.reshape(signals, -1), bank_imag.reshape(signals, -1)], axis=1
    )
    return jnp.concatenate(split_exact(bank), axis=0), jnp.sum(window * window)


def bin_factors(kept_bins, ny):
    fine = 32
    lane = jnp.arange(2 * KY, dtype=jnp.int32)
    chunks = kept_bins.reshape(KY // BINS, 1, BINS)
    bins = jnp.concatenate([chunks, chunks], axis=1).reshape(2 * KY)
    quarter = (lane // BINS % 2) * (ny // 4)
    index = jnp.arange(fine, dtype=jnp.int32)[:, None]
    phase = jnp.stack([index * fine * bins, index * bins + quarter], 0) % ny
    angle = phase.astype(jnp.float32) * (2.0 * math.pi / ny)
    cosine, sine = jnp.cos(angle), jnp.sin(angle)
    return jnp.stack([cosine[0], sine[0], cosine[1], sine[1]], 0)


def body(pressure, centres, strides, kept_bins):
    groups = lax.axis_size("gx")
    rank = lax.axis_index("gx")
    local, nx, ny = pressure.shape
    snaps = local * groups
    half = groups // 2
    each = nx // groups
    radix = 4 if each >= 32 else 2 if each >= 16 else 1
    share = each // radix
    span = nx // radix
    signals = BANDS * OUTS

    partner = rank ^ jnp.arange(half, dtype=jnp.int32)
    times = (partner[:, None] * local + jnp.arange(local, dtype=jnp.int32)[None, :]).reshape(-1)
    factors = bin_factors(kept_bins, ny)
    bank, wsum = filter_bank(centres, strides, snaps, times)
    scale = (1.0 / (OUTS * nx * ny * wsum)).reshape(1)
    rank_word = rank.reshape(1).astype(jnp.int32)

    index = np.arange(span, dtype=np.int64)
    angle = 2.0 * np.pi * (index[:, None] * index[None, :] % span) / span
    mh, ml = split_host(np.concatenate([np.cos(angle), np.sin(-angle)], 1))
    twist = 2.0 * np.pi * (np.arange(radix)[:, None] * index[None, :]) / nx
    twist = np.broadcast_to(twist[:, :, None], (radix, span, BINS))
    twc, tws = np.cos(twist).astype(np.float32), np.sin(-twist).astype(np.float32)

    def whole(shape):
        return pl.BlockSpec(shape, lambda *_: (0,) * len(shape))

    def transform(c, factor, first, count, parts):
        sizes = [2 * share * len(part) for part in parts for _ in range(half)]
        return pl.pallas_call(
            functools.partial(transform_kernel, parts, share, groups),
            grid_spec=pltpu.PrefetchScalarGridSpec(
                num_scalar_prefetch=1,
                grid=(count,),
                in_specs=[
                    pl.BlockSpec((1, nx, ny), lambda t, _: (t + first, 0, 0)),
                    pl.BlockSpec((4, factor.shape[1], LANES), lambda t, _: (0, 0, c)),
                    whole(mh.shape),
                    whole(ml.shape),
                    whole(twc.shape),
                    whole(tws.shape),
                ],
                out_specs=[pl.BlockSpec((1, size, LANES), lambda t, _: (t, 0, 0)) for size in sizes],
                scratch_shapes=[
                    pltpu.VMEM((ny, LANES), jnp.bfloat16),
                    pltpu.VMEM((ny, LANES), jnp.bfloat16),
                    pltpu.VMEM((nx, LANES), jnp.float32),
                    pltpu.VMEM((radix, span, LANES), jnp.float32),
                ],
            ),
            out_shape=[jax.ShapeDtypeStruct((count, size, LANES), jnp.float32) for size in sizes],
            cost_estimate=pl.CostEstimate(
                flops=count * (6 * nx * ny * LANES + 12 * nx * span * LANES),
                bytes_accessed=count * nx * (ny + LANES) * 4,
                transcendentals=0,
            ),
            name="transform",
        )(rank_word, pressure, factor, mh, ml, twc, tws)

    def filtered(bank, places, pieces, side):
        total = pieces[0].shape[1] // 2
        rows = min(16, total)
        blocks = total // rows
        return pl.pallas_call(
            functools.partial(filter_kernel, places),
            grid=(blocks,),
            in_specs=[whole(bank.shape)]
            + [pl.BlockSpec((x.shape[0], rows, LANES), lambda r: (0, side * blocks + r, 0)) for x in pieces],
            out_specs=pl.BlockSpec((rows, signals, LANES), lambda r: (r, 0, 0)),
            out_shape=jax.ShapeDtypeStruct((total, signals, LANES), jnp.float32),
            scratch_shapes=[pltpu.VMEM((half * local * rows, BINS), jnp.float32)] * 2,
            cost_estimate=pl.CostEstimate(
                flops=total * 12 * signals * half * local * LANES,
                bytes_accessed=total * LANES * (half * local + signals) * 4,
                transcendentals=0,
            ),
            name="filter",
        )(bank, *pieces)

    def energy(c, parts, scale, fields, held):
        return pl.pallas_call(
            functools.partial(energy_kernel, parts, share, radix, len(held)),
            in_specs=[pl.BlockSpec(memory_space=pltpu.SMEM)]
            + [pl.BlockSpec(memory_space=pl.ANY)] * len(held)
            + [whole(x.shape) for x in fields],
            out_specs=pl.BlockSpec((BANDS, each, BINS), lambda _: (0, 0, c)),
            out_shape=jax.ShapeDtypeStruct((BANDS, each, KY), jnp.float32),
            scratch_shapes=[pltpu.VMEM((each * BANDS, BINS), jnp.float32)],
            grid=(1,),
            input_output_aliases={1: 0} if held else {},
            name="energy",
        )(scale, *held, *fields)

    def swap(value, bits):
        return lax.ppermute(value, "gx", [(i, i ^ bits) for i in range(groups)])

    def exchange(pieces):
        moved = {}
        moved.update({k: swap(pieces[k], k) for k in range(half // 2, half)})
        moved.update({k: swap(pieces[k], k) for k in range(1, half // 2)})
        return [pieces[0]] + [moved[k] for k in range(1, half)]

    last_made = [rank_word]

    def in_turn(operand):
        return lax.optimization_barrier((operand, last_made[0]))[0]

    def project(c, counts, parts):
        places, found = [], [[] for _ in parts]
        first = 0
        for count in counts:
            made = transform(c, in_turn(factors), first, count, parts)
            last_made[0] = made[0]
            places += [k * local + first for k in range(half)]
            first += count
            for q in range(len(parts)):
                found[q] += exchange(made[q * half : (q + 1) * half])
        return [(places, pieces) for pieces in found]

    def combine(group, side):
        made = filtered(in_turn(bank), *group, side)
        last_made[0] = made
        return made

    def meet(group):
        made = combine(group, 1)
        return swap(made, half)

    everything = (tuple(range(radix)),)
    (zero,) = project(0, first_counts(local), everything)
    parts = last_parts(radix)
    one = project(1, (local,), parts)
    fields = [meet(zero)]
    fields = [combine(zero, 0)] + fields
    rest, out = [], []
    for n, group in enumerate(one):
        theirs = meet(group)
        rest += [combine(group, 0), theirs]
        if n == len(one) // 2:
            out = [energy(0, everything, in_turn(scale), fields, [])]
            last_made[0] = out[0]
    return energy(1, parts, in_turn(scale), rest, out)


def first_counts(local):
    if local % 4 == 0:
        return (local // 4, local // 4, local // 2)
    return (local // 2, local // 2) if local % 2 == 0 else (local,)


def last_parts(radix):
    return {4: ((0, 1), (2,), (3,)), 2: ((0,), (1,)), 1: ((0,),)}[radix]


def solution(mesh):
    return jax.shard_map(
        body,
        mesh=mesh,
        in_specs=(P(("grp", "gx"), None, None), P(), P(), P()),
        out_specs=P("grp", "gx", None),
        check_vma=False,
    )
```
